32 devices in a mesh: rows: 8 (over z, y), cols: 2 (over x), dp: 2 (over core).
Axes of the slice: x: 2, y: 2, z: 4, core: 2. Of those that a mesh axis runs over, the one named last changes fastest.
Arguments:
- queries: bfloat16 [2, 128, 32, 1024], P('dp', 'rows', 'cols'), may hold values from -69 to 69
- keys_values: bfloat16 [2, 2, 128, 32, 1024], P(None, 'dp', 'rows', 'cols'), may hold values from -6 to 6
- out_weight: bfloat16 [1024, 1024], replicated, may hold values from -0.1875 to 0.1875
- out_grad: bfloat16 [2, 128, 32, 1024], P('dp', 'rows', 'cols'), may hold values from -6 to 6
Outputs:
- attn_out: bfloat16 [2, 128, 32, 1024], P('dp', 'rows', 'cols')
- query_grad: bfloat16 [2, 128, 32, 1024], P('dp', 'rows', 'cols')
- kv_grad: bfloat16 [2, 2, 128, 32, 1024], P(None, 'dp', 'rows', 'cols')
- weight_grad: float32 [1024, 1024], P('rows', ('cols', 'dp'))
The draws below stay inside these ranges and needn't reach their ends.
All inputs are finite; a program needn't handle non-finite values.
Results may differ from the reference program's by a relative error of at most 0.012.
The reference program's roundings to bfloat16 on the way count: a program that leaves them out, or rounds other values in their place, can miss the bound.
Values may be sent and summed in bfloat16 or wider, within the bound.
A program may use at most 128 MiB of HBM per device.

```python
import math
import jax
import jax.numpy as jnp
from jax import lax

D = 1024
NH = 16
HD = 64
RAD = 6
WIN = 13
QB = 8
TW = 16
B = 2
HH = 128
WW = 32
TOKENS = 8192


def paired_fields(key):
    shape = (B, HH, WW, NH, HD)
    key_q = jax.random.fold_in(key, 11)
    key_k = jax.random.fold_in(key, 12)
    key_v = jax.random.fold_in(key, 15)
    queries = jnp.clip(jax.random.normal(key_q, shape, jnp.float32), -6.0, 6.0)
    keys = jnp.clip(jax.random.normal(key_k, shape, jnp.float32), -6.0, 6.0)
    values = jnp.clip(jax.random.normal(key_v, shape, jnp.float32), -6.0, 6.0)
    flat = (B, HH, WW, D)
    return (queries.reshape(flat), keys.reshape(flat), values.reshape(flat))


def draw_queries(key, part):
    return paired_fields(key)[0].astype(jnp.bfloat16)


def draw_keys_values(key, part):
    fields = paired_fields(key)
    return jnp.stack((fields[1], fields[2])).astype(jnp.bfloat16)


def with_spikes(array, own_key, source, target, shards_of, factor):
    owner, partner = [(jnp.arange(array.shape[position]) // (array.shape[position] // shards_of)).reshape([-1 if axis == position else 1 for axis in range(array.ndim)]) for position in (source, target)]
    chosen = jax.random.permutation(own_key, shards_of)[partner]
    strong = (owner == chosen) | (owner == (partner + shards_of // 2) % shards_of)
    return jnp.where(strong, factor * array, array)


def block_levels(rng, dims, shards, low, top_value):
    def one(axis_at, blocks):
        draws = jax.random.uniform(jax.random.fold_in(jax.random.fold_in(rng, 6), axis_at), (blocks,), jnp.float32, low / len(shards), top_value / len(shards))
        return jnp.repeat(jnp.exp(draws), dims[axis_at] // blocks).reshape((-1,) + (1,) * (len(dims) - axis_at - 1))

    gain = one(*shards[0])
    for cut in shards[1:]:
        gain = gain * one(*cut)
    return gain


def centred(rng, extent, spread, bound, split=(), kind=jnp.bfloat16):
    array = spread * jax.random.normal(rng, extent, jnp.float32)
    if split:
        array = array * block_levels(rng, extent, split, -0.22, 0.18)
    return jnp.clip(array, -bound, bound).astype(kind)


def bell_draw_with(stream_key, dims, scale, most, split, heavy, kind=jnp.bfloat16):
    result = scale * jax.random.normal(stream_key, dims, jnp.float32)
    if split:
        result = result * block_levels(stream_key, dims, split, -0.22, 0.18)
    return jnp.clip(with_spikes(result, jax.random.fold_in(stream_key, 3), *heavy), -most, most).astype(kind)


def setup_inputs(seed: int = 0) -> dict:
    seeds = jax.random.split(jax.random.key(seed), 5)
    queries = draw_queries(jax.random.fold_in(seeds[4], 71), 0)
    keys_values = draw_keys_values(jax.random.fold_in(seeds[4], 71), 0)
    out_weight = centred(seeds[2], (D, D), D ** -0.5, 0.1875)
    out_grad = bell_draw_with(seeds[3], (B, HH, WW, D), 1.0, 6.0, ((0, 2), (1, 8), (2, 2)), (1, 3, 8, 2.0))
    return dict(queries=queries, keys_values=keys_values, out_weight=out_weight, out_grad=out_grad)


def index_of(*entries):
    return tuple((jnp.asarray(e).astype(jnp.int32) for e in entries))

def window_mask(query_rows, query_cols, key_rows, key_cols, image_h, image_w):
    start_r = jnp.clip(query_rows - RAD, 0, image_h - WIN)
    start_c = jnp.clip(query_cols - RAD, 0, image_w - WIN)
    rows_ok = (key_rows[None, :] >= start_r[:, None]) & (key_rows[None, :] < start_r[:, None] + WIN)
    cols_ok = (key_cols[None, :] >= start_c[:, None]) & (key_cols[None, :] < start_c[:, None] + WIN)
    mask = rows_ok[:, None, :, None] & cols_ok[None, :, None, :]
    return mask.reshape(query_rows.shape[0] * query_cols.shape[0], key_rows.shape[0] * key_cols.shape[0])

def block_core(q_blk, k_blk, v_blk, do_blk, mask):
    scale = 1.0 / math.sqrt(HD)
    q_f = q_blk.astype(jnp.float32).reshape(-1, NH, HD)
    k_f = k_blk.astype(jnp.float32).reshape(-1, NH, HD)
    v_f = v_blk.astype(jnp.float32).reshape(-1, NH, HD)
    do_f = do_blk.astype(jnp.float32).reshape(-1, NH, HD)
    scores = jnp.einsum('qhd,khd->hqk', q_f, k_f) * scale
    scores = jnp.where(mask[None], scores, -jnp.inf)
    top = lax.optimization_barrier(jnp.max(scores, axis=2, keepdims=True))
    expd = jnp.exp(scores - top)
    probs = expd / lax.optimization_barrier(jnp.sum(expd, axis=2, keepdims=True))
    low = lax.optimization_barrier(probs.astype(jnp.bfloat16))
    att = lax.optimization_barrier(jnp.einsum('hqk,khd->qhd', low.astype(jnp.float32), v_f).astype(jnp.bfloat16))
    delta = lax.optimization_barrier(jnp.sum(do_f * att.astype(jnp.float32), axis=2))
    dprob = jnp.einsum('qhd,khd->hqk', do_f, v_f)
    dlow = lax.optimization_barrier((probs * (dprob - delta.T[:, :, None]) * scale).astype(jnp.bfloat16))
    dq = jnp.einsum('hqk,khd->qhd', dlow.astype(jnp.float32), k_f).astype(jnp.bfloat16)
    dk = jnp.einsum('hqk,qhd->khd', dlow.astype(jnp.float32), q_f)
    dv = jnp.einsum('hqk,qhd->khd', low.astype(jnp.float32), do_f)
    width = q_blk.shape[1]
    return (att.reshape(-1, width), dq.reshape(-1, width), dk.reshape(-1, width), dv.reshape(-1, width))

def one_image(queries, keys, values, out_grad, out_weight):
    key_pad = jnp.pad(keys, ((RAD, RAD), (RAD, RAD), (0, 0)))
    val_pad = jnp.pad(values, ((RAD, RAD), (RAD, RAD), (0, 0)))
    grad_rows = out_grad.reshape(-1, D)
    d_att = jnp.dot(grad_rows, out_weight.T, preferred_element_type=jnp.float32).astype(jnp.bfloat16).reshape(HH, WW, D)
    row_blocks = HH // QB
    col_blocks = WW // TW
    key_h = QB + 2 * RAD
    key_w = TW + 2 * RAD

    def step(accum, index):
        row = (index // col_blocks * QB).astype(jnp.int32)
        col = (index % col_blocks * TW).astype(jnp.int32)
        lower = jnp.clip(row - RAD, 0, HH - QB - 2 * RAD).astype(jnp.int32)
        q_blk = lax.dynamic_slice(queries, index_of(row, col, 0), (QB, TW, D)).reshape(-1, D)
        do_blk = lax.dynamic_slice(d_att, index_of(row, col, 0), (QB, TW, D)).reshape(-1, D)
        k_blk = lax.dynamic_slice(key_pad, index_of(lower + RAD, col, 0), (key_h, key_w, D)).reshape(-1, D)
        v_blk = lax.dynamic_slice(val_pad, index_of(lower + RAD, col, 0), (key_h, key_w, D)).reshape(-1, D)
        mask = window_mask(row + jnp.arange(QB, dtype=jnp.int32), col + jnp.arange(TW, dtype=jnp.int32), lower + jnp.arange(key_h, dtype=jnp.int32), col - RAD + jnp.arange(key_w, dtype=jnp.int32), HH, WW)
        att, dq, dk, dv = block_core(q_blk, k_blk, v_blk, do_blk, mask)
        older = lax.dynamic_slice(accum, index_of(0, lower + RAD, col, 0), (2, key_h, key_w, D))
        newer = older + jnp.stack((dk, dv)).reshape(2, key_h, key_w, D)
        accum = lax.dynamic_update_slice(accum, newer, index_of(0, lower + RAD, col, 0))
        return (accum, (att, dq))
    start = jnp.zeros((2, HH + 2 * RAD, WW + 2 * RAD, D), jnp.float32)
    accum, (att_blocks, dq_blocks) = lax.scan(step, start, jnp.arange(row_blocks * col_blocks, dtype=jnp.int32))
    attended = att_blocks.reshape(row_blocks, col_blocks, QB, TW, D).transpose(0, 2, 1, 3, 4).reshape(HH, WW, D)
    query_grad = dq_blocks.reshape(row_blocks, col_blocks, QB, TW, D).transpose(0, 2, 1, 3, 4).reshape(HH, WW, D)
    kv_grad = accum[:, RAD:RAD + HH, RAD:RAD + WW].astype(jnp.bfloat16)
    flat_att = attended.reshape(-1, D)
    attn_out = jnp.dot(flat_att, out_weight, preferred_element_type=jnp.float32).astype(jnp.bfloat16).reshape(HH, WW, D)
    weight_term = jnp.dot(flat_att.T, grad_rows, preferred_element_type=jnp.float32)
    return (attn_out, query_grad, kv_grad, weight_term)

def reference(queries, keys_values, out_weight, out_grad):
    results = [one_image(queries[b], keys_values[0, b], keys_values[1, b], out_grad[b], out_weight) for b in range(B)]
    attn_out = jnp.stack([r[0] for r in results])
    query_grad = jnp.stack([r[1] for r in results])
    kv_grad = jnp.stack([r[2] for r in results], axis=1)
    total = results[0][3]
    for r in results[1:]:
        total = total + r[3]
    weight_grad = total * (1.0 / math.sqrt(TOKENS))
    return (attn_out, query_grad, kv_grad, weight_grad)
```

```python
import functools
import math

import jax
import jax.numpy as jnp
from jax import lax
from jax.experimental import pallas as pl
from jax.experimental.pallas import tpu as pltpu
from jax.sharding import PartitionSpec as P

NH = 16
HD = 64
RAD = 6
WIN = 13
QB = 8
PAIR = 2 * HD
GROUP = QB * RAD
MESH = pl.DeviceIdType.MESH
F32 = jnp.float32
BF16 = jnp.bfloat16


def mm(a, b, ca, cb):
    return lax.dot_general(a, b, (((ca,), (cb,)), ((), ())), preferred_element_type=F32)


def kernel(
    tile_h, tile_w, n_rows, n_cols, n_dp,
    q_ref, kv_ref, w_ref, og_ref,
    out_ref, dq_ref, kvg_ref, wg_ref,
    main, strip, sstrip, acc, sacc, bias, probs, att_t, d_att,
    rim_out, rim_in, srim_out, srim_in,
    slab, slab_low, got_dp, low_cols, got_cols, low_rows, got_rows,
    halo_send, halo_recv, rim_send, rim_recv, sum_send, sum_recv,
):
    sides = strip.shape[0]
    blocks = tile_h // QB
    tokens = tile_h * tile_w
    width = q_ref.shape[1]
    pairs = width // PAIR
    edge = RAD * tile_w
    span = (QB + 2 * RAD) * tile_w
    sspan = 3 * GROUP
    step = QB * tile_w
    image_h, image_w = tile_h * n_rows, tile_w * n_cols
    scale = 1.0 / math.sqrt(HD)
    r, c, d = lax.axis_index("rows"), lax.axis_index("cols"), lax.axis_index("dp")

    links = [(-1, None), (1, None)] + [(dr, s) for s in range(sides) for dr in (0, -1, 1)]

    def partner(dr, s):
        if s is None:
            col = c
        elif sides == 1:
            col = 1 - c
        else:
            col = c + (2 * s - 1)
        return {"rows": r + dr, "cols": col}

    def there(dr, s):
        ok = None
        if dr:
            ok = r > 0 if dr < 0 else r < n_rows - 1
        if s is not None and sides == 2:
            side_ok = c > 0 if s == 0 else c < n_cols - 1
            ok = side_ok if ok is None else ok & side_ok
        return ok

    def guarded(dr, s, action):
        ok = there(dr, s)
        if ok is None:
            action()
        else:
            pl.when(ok)(action)

    def slot(s):
        return 0 if sides == 1 else 1 - s

    def starts_at(s):
        if sides == 1:
            return (1 - c) * (tile_w - RAD)
        return 0 if s == 0 else tile_w - RAD

    barrier = pltpu.get_barrier_semaphore()
    for k in range(1, n_rows):
        pl.semaphore_signal(barrier, 1, device_id={"rows": lax.rem(r + k, n_rows)}, device_id_type=MESH)
    for k in range(1, n_cols):
        pl.semaphore_signal(barrier, 1, device_id={"cols": lax.rem(c + k, n_cols)}, device_id_type=MESH)
    for k in range(1, n_dp):
        pl.semaphore_signal(barrier, 1, device_id={"dp": lax.rem(d + k, n_dp)}, device_id_type=MESH)
    greeted = n_rows + n_cols + n_dp - 3
    for dr, s in links:
        if dr and s is not None:
            def greet(dr=dr, s=s):
                pl.semaphore_signal(barrier, 1, device_id=partner(dr, s), device_id_type=MESH)
            guarded(dr, s, greet)
            greeted = greeted + there(dr, s).astype(jnp.int32)

    strip_tokens = tile_h * RAD

    def pick(n, s):
        token = lax.broadcasted_iota(jnp.int32, (n, tokens), 0)
        row = (token * 10923) >> 16
        col = token - row * RAD
        place = row * tile_w + col + starts_at(s)
        return (place == lax.broadcasted_iota(jnp.int32, (n, tokens), 1)).astype(F32).astype(BF16)

    def scatter(s):
        shape = (tokens, GROUP * (blocks + 2))
        token = lax.broadcasted_iota(jnp.int32, shape, 1)
        row = (token * 10923) >> 16
        col = token - row * RAD
        row = row - jnp.where(row < QB, 0, jnp.where(row < QB + tile_h, QB, 2 * QB))
        place = row * tile_w + col + starts_at(s)
        return (place == lax.broadcasted_iota(jnp.int32, shape, 0)).astype(F32).astype(BF16)

    for s in range(sides):
        chosen = pick(strip_tokens, s)
        for k in range(2):
            sstrip[s, k] = mm(chosen, kv_ref[k], 1, 0).astype(BF16)

    pl.semaphore_wait(barrier, greeted)

    def halo_copy(index):
        dr, s = links[index]
        if s is None:
            if dr < 0:
                src, dst = kv_ref.at[:, pl.ds(0, edge)], main.at[:, pl.ds(edge + tokens, edge)]
            else:
                src, dst = kv_ref.at[:, pl.ds(tokens - edge, edge)], main.at[:, pl.ds(0, edge)]
        else:
            own, far = sstrip.at[s], strip.at[slot(s)]
            if dr == 0:
                src, dst = own, far.at[:, pl.ds(GROUP, strip_tokens)]
            elif dr < 0:
                src, dst = own.at[:, pl.ds(0, GROUP)], far.at[:, pl.ds(GROUP + strip_tokens, GROUP)]
            else:
                src, dst = own.at[:, pl.ds(strip_tokens - GROUP, GROUP)], far.at[:, pl.ds(0, GROUP)]
        return src, dst

    def rim_copy(index):
        dr, s = links[index]
        if s is None:
            at = 0 if dr < 0 else 1
            return rim_out.at[at], rim_in.at[1 - at]
        own, far = srim_out.at[s], srim_in.at[slot(s)]
        if dr == 0:
            return own.at[:, pl.ds(GROUP, strip_tokens)], far.at[:, pl.ds(GROUP, strip_tokens)]
        if dr < 0:
            return own.at[:, pl.ds(0, GROUP)], far.at[:, pl.ds(GROUP + strip_tokens, GROUP)]
        return own.at[:, pl.ds(GROUP + strip_tokens, GROUP)], far.at[:, pl.ds(0, GROUP)]

    def mirror(index):
        dr, s = links[index]
        return links.index((-dr, None if s is None else (s if sides == 1 else 1 - s)))

    def remote(copy, index, send, recv):
        src, dst = copy(index)
        return pltpu.make_async_remote_copy(
            src_ref=src, dst_ref=dst, send_sem=send.at[index], recv_sem=recv.at[mirror(index)],
            device_id=partner(*links[index]), device_id_type=MESH,
        )

    def start_all(copy, send, recv):
        for index in range(len(links)):
            guarded(*links[index], lambda index=index: remote(copy, index, send, recv).start())

    def wait_all(copy, send, recv):
        for index in range(len(links)):
            def action(index=index):
                src, dst = copy(mirror(index))
                pltpu.make_async_remote_copy(
                    src_ref=src, dst_ref=dst, send_sem=send.at[index], recv_sem=recv.at[index],
                    device_id=partner(*links[index]), device_id_type=MESH,
                ).wait_recv()
                remote(copy, index, send, recv).wait_send()
            guarded(*links[index], action)

    start_all(halo_copy, halo_send, halo_recv)

    for index in range(len(links)):
        ok = there(*links[index])
        if ok is not None:
            def clear(index=index):
                dst = halo_copy(mirror(index))[1]
                dst[...] = jnp.zeros(dst.shape, BF16)
                dst = rim_copy(mirror(index))[1]
                dst[...] = jnp.zeros(dst.shape, BF16)
            pl.when(jnp.logical_not(ok))(clear)

    for k in range(2):
        main[k, edge : edge + tokens] = kv_ref[k]

    d_att[...] = mm(og_ref[...], w_ref[...], 1, 1).astype(BF16)
    acc[...] = jnp.zeros(acc.shape, F32)
    sacc[...] = jnp.zeros(sacc.shape, F32)

    def put_bias(b, at, rows, cols, n):
        lane = lax.broadcasted_iota(jnp.int32, (n, step), 1)
        q_row = r * tile_h + b * QB + lane // tile_w
        q_col = c * tile_w + lane % tile_w
        first_r = jnp.clip(q_row - RAD, 0, image_h - WIN)
        first_c = jnp.clip(q_col - RAD, 0, image_w - WIN)
        ok = (rows >= first_r) & (rows < first_r + WIN) & (cols >= first_c) & (cols < first_c + WIN)
        bias[b, at : at + n] = jnp.where(ok, 0.0, -1e30)

    for b in range(blocks):
        token = lax.broadcasted_iota(jnp.int32, (span, step), 0)
        put_bias(b, 0, r * tile_h + b * QB - RAD + token // tile_w, c * tile_w + token % tile_w, span)
        token = lax.broadcasted_iota(jnp.int32, (sspan, step), 0)
        row = (token * 10923) >> 16
        for s in range(sides):
            if sides == 1:
                first = c * tile_w + jnp.where(c == 0, tile_w, -RAD)
            else:
                first = c * tile_w + (tile_w if s else -RAD)
            put_bias(
                b, span + s * sspan, r * tile_h + (b - 1) * QB + row, first + token - row * RAD, sspan
            )

    wait_all(halo_copy, halo_send, halo_recv)

    def lanes(p):
        return pl.ds(pl.multiple_of(p * PAIR, PAIR), PAIR)

    def keys_of(k, b, p):
        parts = [main[k, step * b : step * b + span, lanes(p)]]
        for s in range(sides):
            parts.append(strip[s, k, GROUP * b : GROUP * b + sspan, lanes(p)])
        return jnp.concatenate(parts, axis=0)

    def split_heads(x):
        low_head = lax.broadcasted_iota(jnp.int32, x.shape, 1) < HD
        wide = x.astype(F32)
        return jnp.concatenate(
            [jnp.where(low_head, wide, 0.0), jnp.where(low_head, 0.0, wide)], axis=0
        ).astype(BF16)

    def queries_of(b, p):
        return split_heads(q_ref[step * b : step * (b + 1), lanes(p)].astype(F32) * scale)

    def scores_of(keys, b, p):
        hidden = bias[b]
        return mm(keys, queries_of(b, p), 1, 1) + jnp.concatenate([hidden, hidden], axis=1)

    keep = probs.shape[1] == span + sides * sspan

    def own_heads(x):
        return jnp.concatenate([x[:HD, :step], x[HD:, step:]], axis=0)

    for b in range(blocks):
        def forward(p, carry, b=b):
            keys, values = keys_of(0, b, p), keys_of(1, b, p)
            scores = scores_of(keys, b, p)
            top = jnp.max(scores, axis=0, keepdims=True)
            expd = jnp.exp(scores - top)
            share = 1.0 / jnp.sum(expd, axis=0, keepdims=True)
            full = expd * share
            if keep:
                probs[b * pairs + p] = full
            else:
                probs[b * pairs + p, 0:1] = top
                probs[b * pairs + p, 1:2] = share
            att = own_heads(mm(values, full.astype(BF16), 0, 0)).astype(BF16)
            att_t[pl.ds(pl.multiple_of(p * PAIR, PAIR), PAIR), step * b : step * (b + 1)] = att
            return carry

        lax.fori_loop(0, pairs, forward, 0)

    block_c = slab.shape[3]
    rows_c = width // n_rows
    og = og_ref[...]
    for j in range(n_cols):
        for e in range(n_dp):
            at = (j * n_dp + e) * block_c
            product = mm(att_t[...], og[:, at : at + block_c], 1, 0)
            slab[e, j] = product
            slab_low[e, j] = product.astype(BF16)

    def dp_copy(k):
        to = lax.rem(d + k, n_dp)
        return pltpu.make_async_remote_copy(
            src_ref=slab_low.at[to], dst_ref=got_dp.at[k - 1],
            send_sem=sum_send.at[0, k - 1], recv_sem=sum_recv.at[0, k - 1],
            device_id={"dp": to}, device_id_type=MESH,
        )

    def cols_copy(k):
        to = lax.rem(c + k, n_cols)
        return pltpu.make_async_remote_copy(
            src_ref=low_cols.at[to], dst_ref=got_cols.at[k - 1],
            send_sem=sum_send.at[1, k - 1], recv_sem=sum_recv.at[1, k - 1],
            device_id={"cols": to}, device_id_type=MESH,
        )

    def rows_copy(k):
        to = lax.rem(r + k, n_rows)
        return pltpu.make_async_remote_copy(
            src_ref=low_rows.at[to], dst_ref=got_rows.at[k - 1],
            send_sem=sum_send.at[2, k - 1], recv_sem=sum_recv.at[2, k - 1],
            device_id={"rows": to}, device_id_type=MESH,
        )

    for k in range(1, n_dp):
        dp_copy(k).start()
    out_ref[...] = mm(att_t[...], w_ref[...], 0, 0).astype(BF16)

    for b in range(blocks):
        def backward(p, carry, b=b):
            keys, values = keys_of(0, b, p), keys_of(1, b, p)
            d_blk = d_att[step * b : step * (b + 1), lanes(p)]
            d_two = split_heads(d_blk)
            att = att_t[pl.ds(pl.multiple_of(p * PAIR, PAIR), PAIR), step * b : step * (b + 1)]
            both = d_blk.astype(F32).T * att.astype(F32)
            delta = jnp.concatenate(
                [
                    jnp.sum(both[:HD], axis=0, keepdims=True),
                    jnp.sum(both[HD:], axis=0, keepdims=True),
                ],
                axis=1,
            )
            if keep:
                full = probs[b * pairs + p]
            else:
                top, share = probs[b * pairs + p, 0:1], probs[b * pairs + p, 1:2]
                full = jnp.exp(scores_of(keys, b, p) - top) * share
            dscores = (full * (mm(values, d_two, 1, 1) - delta)).astype(BF16)
            dq = own_heads(mm(keys, dscores, 0, 0)) * scale
            dq_ref[step * b : step * (b + 1), lanes(p)] = dq.T.astype(BF16)
            for k, grad in (
                (0, mm(dscores, queries_of(b, p), 1, 0)),
                (1, mm(full.astype(BF16), d_two, 1, 0)),
            ):
                acc[k, step * b : step * b + span, lanes(p)] += grad[:span]
                for s in range(sides):
                    at = span + s * sspan
                    sacc[s, k, GROUP * b : GROUP * b + sspan, lanes(p)] += grad[at : at + sspan]
            return carry

        lax.fori_loop(0, pairs, backward, 0)
        if b == 0:
            for k in range(1, n_dp):
                dp_copy(k).wait()
            for j in range(n_cols):
                total = slab[d, j]
                for k in range(1, n_dp):
                    total = total + got_dp[k - 1, j].astype(F32)
                slab[d, j] = total
                low_cols[j] = total.astype(BF16)
            for k in range(1, n_cols):
                cols_copy(k).start()

    for k in range(2):
        rim_out[0, k] = acc[k, :edge].astype(BF16)
        rim_out[1, k] = acc[k, edge + tokens :].astype(BF16)
        for s in range(sides):
            srim_out[s, k] = sacc[s, k].astype(BF16)
    start_all(rim_copy, rim_send, rim_recv)

    for k in range(1, n_cols):
        cols_copy(k).wait()
    total = slab[d, c]
    for k in range(1, n_cols):
        total = total + got_cols[k - 1].astype(F32)
    slab[d, c] = total
    for i in range(n_rows):
        low_rows[i] = total[i * rows_c : (i + 1) * rows_c].astype(BF16)
    for k in range(1, n_rows):
        rows_copy(k).start()

    wait_all(rim_copy, rim_send, rim_recv)
    for k in range(2):
        own = acc[k, edge : edge + tokens]
        for s in range(sides):
            own = own + mm(scatter(s), srim_in[s, k], 1, 0)
        acc[k, edge : edge + tokens] = own
        acc[k, edge : 2 * edge] += rim_in[0, k].astype(F32)
        acc[k, tokens : edge + tokens] += rim_in[1, k].astype(F32)
        kvg_ref[k] = acc[k, edge : edge + tokens].astype(BF16)

    for k in range(1, n_rows):
        rows_copy(k).wait()
    total = slab[d, c, pl.ds(pl.multiple_of(r * rows_c, rows_c), rows_c)]
    for k in range(1, n_rows):
        total = total + got_rows[k - 1].astype(F32)
    wg_ref[...] = total * (1.0 / math.sqrt(image_h * image_w * n_dp))


def local(n_rows, n_cols, n_dp, queries, keys_values, out_weight, out_grad):
    tile_h, tile_w, width = queries.shape[1:]
    tokens = tile_h * tile_w
    sides = 1 if n_cols == 2 else 2
    blocks = tile_h // QB
    pairs = width // PAIR
    edge = RAD * tile_w
    grown = tokens + 2 * edge
    sgrown = GROUP * (blocks + 2)
    seen = (QB + 2 * RAD) * tile_w + sides * 3 * GROUP
    step = QB * tile_w
    keep = blocks * pairs * seen * 2 * step * 4 < 12 * 2**20
    block_c = width // (n_cols * n_dp)
    rows_c = width // n_rows
    links = 2 + 3 * sides
    most = max(n_rows, n_cols, n_dp) - 1
    vmem = pl.BlockSpec(memory_space=pltpu.VMEM)
    dma = pltpu.SemaphoreType.DMA
    out, dq, kvg, wg = pl.pallas_call(
        functools.partial(kernel, tile_h, tile_w, n_rows, n_cols, n_dp),
        out_shape=(
            jax.ShapeDtypeStruct((tokens, width), BF16),
            jax.ShapeDtypeStruct((tokens, width), BF16),
            jax.ShapeDtypeStruct((2, tokens, width), BF16),
            jax.ShapeDtypeStruct((rows_c, block_c), F32),
        ),
        in_specs=[vmem] * 4,
        out_specs=(vmem,) * 4,
        scratch_shapes=[
            pltpu.VMEM((2, grown, width), BF16),
            pltpu.VMEM((sides, 2, sgrown, width), BF16),
            pltpu.VMEM((sides, 2, tile_h * RAD, width), BF16),
            pltpu.VMEM((2, grown, width), F32),
            pltpu.VMEM((sides, 2, sgrown, width), F32),
            pltpu.VMEM((blocks, seen, step), F32),
            pltpu.VMEM((blocks * pairs, seen if keep else 8, 2 * step), F32),
            pltpu.VMEM((width, tokens), BF16),
            pltpu.VMEM((tokens, width), BF16),
            pltpu.VMEM((2, 2, edge, width), BF16),
            pltpu.VMEM((2, 2, edge, width), BF16),
            pltpu.VMEM((sides, 2, sgrown, width), BF16),
            pltpu.VMEM((sides, 2, sgrown, width), BF16),
            pltpu.VMEM((n_dp, n_cols, width, block_c), F32),
            pltpu.VMEM((n_dp, n_cols, width, block_c), BF16),
            pltpu.VMEM((n_dp - 1, n_cols, width, block_c), BF16),
            pltpu.VMEM((n_cols, width, block_c), BF16),
            pltpu.VMEM((n_cols - 1, width, block_c), BF16),
            pltpu.VMEM((n_rows, rows_c, block_c), BF16),
            pltpu.VMEM((n_rows - 1, rows_c, block_c), BF16),
            dma((links,)), dma((links,)), dma((links,)), dma((links,)),
            dma((3, most)), dma((3, most)),
        ],
        compiler_params=pltpu.CompilerParams(
            collective_id=0, has_side_effects=True, vmem_limit_bytes=60 * 2**20
        ),
    )(
        queries.reshape(tokens, width),
        keys_values.reshape(2, tokens, width),
        out_weight,
        out_grad.reshape(tokens, width),
    )
    return (
        out.reshape(queries.shape),
        dq.reshape(queries.shape),
        kvg.reshape(keys_values.shape),
        wg,
    )


def solution(mesh):
    in_specs = (
        P("dp", "rows", "cols", None),
        P(None, "dp", "rows", "cols", None),
        P(),
        P("dp", "rows", "cols", None),
    )
    out_specs = (
        P("dp", "rows", "cols", None),
        P("dp", "rows", "cols", None),
        P(None, "dp", "rows", "cols", None),
        P("rows", ("cols", "dp")),
    )
    sizes = (mesh.shape["rows"], mesh.shape["cols"], mesh.shape["dp"])
    return jax.shard_map(
        functools.partial(local, *sizes),
        mesh=mesh, in_specs=in_specs, out_specs=out_specs, check_vma=False,
    )
```

```python
import functools
import math

import jax
import jax.numpy as jnp
from jax import lax
from jax.experimental import pallas as pl
from jax.experimental.pallas import tpu as pltpu
from jax.sharding import PartitionSpec as P

NH = 16
HD = 64
RAD = 6
WIN = 13
QB = 8
PAIR = 2 * HD
CHUNK = 2
GROUP = QB * RAD
MESH = pl.DeviceIdType.MESH
F32 = jnp.float32
BF16 = jnp.bfloat16


def mm(a, b, ca, cb):
    return lax.dot_general(a, b, (((ca,), (cb,)), ((), ())), preferred_element_type=F32)


def kernel(
    tile_h, tile_w, n_rows, n_cols, n_dp,
    q_ref, kv_ref, w_ref, og_ref,
    out_ref, dq_ref, kvg_ref, wg_ref,
    main, strip, sstrip, acc, sacc, bias, att_t, d_att,
    rim_out, rim_in, srim_out, srim_in,
    slab, slab_low, got_dp, low_cols, got_cols, low_rows, got_rows,
    halo_send, halo_recv, rim_send, rim_recv, dp_sems, cols_sems, rows_sems,
):
    sides = strip.shape[0]
    blocks = tile_h // QB
    tokens = tile_h * tile_w
    width = q_ref.shape[1]
    pairs = width // PAIR
    edge = RAD * tile_w
    span = (QB + 2 * RAD) * tile_w
    sspan = 3 * GROUP
    step = QB * tile_w
    image_h, image_w = tile_h * n_rows, tile_w * n_cols
    scale = 1.0 / math.sqrt(HD)
    r, c, d = lax.axis_index("rows"), lax.axis_index("cols"), lax.axis_index("dp")

    links = [(-1, None), (1, None)] + [(dr, s) for s in range(sides) for dr in (0, -1, 1)]

    def partner(dr, s):
        if s is None:
            col = c
        elif sides == 1:
            col = 1 - c
        else:
            col = c + (2 * s - 1)
        return {"rows": r + dr, "cols": col}

    def there(dr, s):
        ok = None
        if dr:
            ok = r > 0 if dr < 0 else r < n_rows - 1
        if s is not None and sides == 2:
            side_ok = c > 0 if s == 0 else c < n_cols - 1
            ok = side_ok if ok is None else ok & side_ok
        return ok

    def guarded(dr, s, action):
        ok = there(dr, s)
        if ok is None:
            action()
        else:
            pl.when(ok)(action)

    def slot(s):
        return 0 if sides == 1 else 1 - s

    def starts_at(s):
        if sides == 1:
            return (1 - c) * (tile_w - RAD)
        return 0 if s == 0 else tile_w - RAD

    barrier = pltpu.get_barrier_semaphore()
    for k in range(1, n_rows):
        pl.semaphore_signal(barrier, 1, device_id={"rows": lax.rem(r + k, n_rows)}, device_id_type=MESH)
    for k in range(1, n_cols):
        pl.semaphore_signal(barrier, 1, device_id={"cols": lax.rem(c + k, n_cols)}, device_id_type=MESH)
    for k in range(1, n_dp):
        pl.semaphore_signal(barrier, 1, device_id={"dp": lax.rem(d + k, n_dp)}, device_id_type=MESH)
    greeted = n_rows + n_cols + n_dp - 3
    for dr, s in links:
        if dr and s is not None:
            def greet(dr=dr, s=s):
                pl.semaphore_signal(barrier, 1, device_id=partner(dr, s), device_id_type=MESH)
            guarded(dr, s, greet)
            greeted = greeted + there(dr, s).astype(jnp.int32)

    strip_tokens = tile_h * RAD

    def pick(n, s):
        token = lax.broadcasted_iota(jnp.int32, (n, tokens), 0)
        row = (token * 10923) >> 16
        col = token - row * RAD
        place = row * tile_w + col + starts_at(s)
        return (place == lax.broadcasted_iota(jnp.int32, (n, tokens), 1)).astype(F32).astype(BF16)

    def scatter(s):
        shape = (tokens, GROUP * (blocks + 2))
        token = lax.broadcasted_iota(jnp.int32, shape, 1)
        row = (token * 10923) >> 16
        col = token - row * RAD
        row = row - jnp.where(row < QB, 0, jnp.where(row < QB + tile_h, QB, 2 * QB))
        place = row * tile_w + col + starts_at(s)
        return (place == lax.broadcasted_iota(jnp.int32, shape, 0)).astype(F32).astype(BF16)

    for s in range(sides):
        chosen = pick(strip_tokens, s)
        for k in range(2):
            sstrip[s, k] = mm(chosen, kv_ref[k], 1, 0).astype(BF16)

    pl.semaphore_wait(barrier, greeted)

    chunks = pairs // CHUNK
    part = CHUNK * PAIR

    def halo_copy(index, at):
        dr, s = links[index]
        if s is None:
            if dr < 0:
                return kv_ref.at[:, pl.ds(0, edge), at], main.at[:, pl.ds(edge + tokens, edge), at]
            return kv_ref.at[:, pl.ds(tokens - edge, edge), at], main.at[:, pl.ds(0, edge), at]
        own, far = sstrip.at[s], strip.at[slot(s)]
        if dr == 0:
            return own.at[:, :, at], far.at[:, pl.ds(GROUP, strip_tokens), at]
        if dr < 0:
            return own.at[:, pl.ds(0, GROUP), at], far.at[:, pl.ds(GROUP + strip_tokens, GROUP), at]
        return own.at[:, pl.ds(strip_tokens - GROUP, GROUP), at], far.at[:, pl.ds(0, GROUP), at]

    def rim_copy(index, at):
        dr, s = links[index]
        if s is None:
            way = 0 if dr < 0 else 1
            return rim_out.at[way, :, :, at], rim_in.at[1 - way, :, :, at]
        own, far = srim_out.at[s], srim_in.at[slot(s)]
        if dr == 0:
            which = pl.ds(GROUP, strip_tokens)
            return own.at[:, which, at], far.at[:, which, at]
        first, last = pl.ds(0, GROUP), pl.ds(GROUP + strip_tokens, GROUP)
        if dr < 0:
            return own.at[:, first, at], far.at[:, last, at]
        return own.at[:, last, at], far.at[:, first, at]

    def mirror(index):
        dr, s = links[index]
        return links.index((-dr, None if s is None else (s if sides == 1 else 1 - s)))

    def remote(copy, index, g, send, recv):
        src, dst = copy(index, pl.ds(g * part, part))
        return pltpu.make_async_remote_copy(
            src_ref=src, dst_ref=dst, send_sem=send.at[index, g], recv_sem=recv.at[mirror(index), g],
            device_id=partner(*links[index]), device_id_type=MESH,
        )

    def start_all(copy, g, send, recv):
        for index in range(len(links)):
            guarded(*links[index], lambda index=index: remote(copy, index, g, send, recv).start())

    def wait_all(copy, g, send, recv):
        for index in range(len(links)):
            def action(index=index):
                src, dst = copy(mirror(index), pl.ds(g * part, part))
                pltpu.make_async_remote_copy(
                    src_ref=src, dst_ref=dst, send_sem=send.at[index, g], recv_sem=recv.at[index, g],
                    device_id=partner(*links[index]), device_id_type=MESH,
                ).wait_recv()
                remote(copy, index, g, send, recv).wait_send()
            guarded(*links[index], action)

    for g in range(chunks):
        start_all(halo_copy, g, halo_send, halo_recv)

    for index in range(len(links)):
        ok = there(*links[index])
        if ok is not None:
            def clear(index=index):
                dst = halo_copy(mirror(index), pl.ds(0, width))[1]
                dst[...] = jnp.zeros(dst.shape, BF16)
                dst = rim_copy(mirror(index), pl.ds(0, width))[1]
                dst[...] = jnp.zeros(dst.shape, BF16)
            pl.when(jnp.logical_not(ok))(clear)

    for k in range(2):
        main[k, edge : edge + tokens] = kv_ref[k]
    got_rows[r] = jnp.zeros(got_rows.shape[1:], BF16)

    d_att[...] = mm(og_ref[...], w_ref[...], 1, 1).astype(BF16)
    acc[...] = jnp.zeros(acc.shape, F32)
    sacc[...] = jnp.zeros(sacc.shape, F32)

    def put_bias(b, at, rows, cols, n):
        lane = lax.broadcasted_iota(jnp.int32, (n, step), 1)
        q_row = r * tile_h + b * QB + lane // tile_w
        q_col = c * tile_w + lane % tile_w
        first_r = jnp.clip(q_row - RAD, 0, image_h - WIN)
        first_c = jnp.clip(q_col - RAD, 0, image_w - WIN)
        ok = (rows >= first_r) & (rows < first_r + WIN) & (cols >= first_c) & (cols < first_c + WIN)
        bias[b, at : at + n] = jnp.where(ok, 0.0, -1e30)

    for b in range(blocks):
        token = lax.broadcasted_iota(jnp.int32, (span, step), 0)
        put_bias(b, 0, r * tile_h + b * QB - RAD + token // tile_w, c * tile_w + token % tile_w, span)
        token = lax.broadcasted_iota(jnp.int32, (sspan, step), 0)
        row = (token * 10923) >> 16
        for s in range(sides):
            if sides == 1:
                first = c * tile_w + jnp.where(c == 0, tile_w, -RAD)
            else:
                first = c * tile_w + (tile_w if s else -RAD)
            put_bias(
                b, span + s * sspan, r * tile_h + (b - 1) * QB + row, first + token - row * RAD, sspan
            )

    def lanes(p):
        return pl.ds(pl.multiple_of(p * PAIR, PAIR), PAIR)

    def keys_of(k, b, p):
        parts = [main[k, step * b : step * b + span, lanes(p)]]
        for s in range(sides):
            parts.append(strip[s, k, GROUP * b : GROUP * b + sspan, lanes(p)])
        return jnp.concatenate(parts, axis=0)

    def split_heads(x):
        low_head = lax.broadcasted_iota(jnp.int32, x.shape, 1) < HD
        wide = x.astype(F32)
        return jnp.concatenate(
            [jnp.where(low_head, wide, 0.0), jnp.where(low_head, 0.0, wide)], axis=0
        ).astype(BF16)

    def queries_of(b, p):
        return split_heads(q_ref[step * b : step * (b + 1), lanes(p)].astype(F32) * scale)

    def own_heads(x):
        return jnp.concatenate([x[:HD, :step], x[HD:, step:]], axis=0)

    def attend(p, carry):
        for b in range(blocks):
            here = slice(step * b, step * (b + 1))
            keys, values = keys_of(0, b, p), keys_of(1, b, p)
            q_two = queries_of(b, p)
            d_blk = d_att[here, lanes(p)]
            d_two = split_heads(d_blk)
            hidden = bias[b]
            scores = mm(keys, q_two, 1, 1) + jnp.concatenate([hidden, hidden], axis=1)
            expd = jnp.exp(scores - jnp.max(scores, axis=0, keepdims=True))
            full = expd * (1.0 / jnp.sum(expd, axis=0, keepdims=True))
            low = full.astype(BF16)
            att = own_heads(mm(values, low, 0, 0)).astype(BF16)
            att_t[lanes(p), here] = att
            both = d_blk.astype(F32).T * att.astype(F32)
            delta = jnp.concatenate(
                [
                    jnp.sum(both[:HD], axis=0, keepdims=True),
                    jnp.sum(both[HD:], axis=0, keepdims=True),
                ],
                axis=1,
            )
            dscores = (full * (mm(values, d_two, 1, 1) - delta)).astype(BF16)
            dq = own_heads(mm(keys, dscores, 0, 0)) * scale
            dq_ref[here, lanes(p)] = dq.T.astype(BF16)
            for k, grad in ((0, mm(dscores, q_two, 1, 0)), (1, mm(low, d_two, 1, 0))):
                acc[k, step * b : step * b + span, lanes(p)] += grad[:span]
                for s in range(sides):
                    at = span + s * sspan
                    sacc[s, k, GROUP * b : GROUP * b + sspan, lanes(p)] += grad[at : at + sspan]
        return carry

    block_c = slab.shape[3]
    rows_c = width // n_rows
    og = og_ref[...]

    def dp_copy(k, g):
        to = lax.rem(d + k, n_dp)
        at = pl.ds(g * part, part)
        return pltpu.make_async_remote_copy(
            src_ref=slab_low.at[to, :, at], dst_ref=got_dp.at[k - 1, :, at],
            send_sem=dp_sems.at[0, k - 1, g], recv_sem=dp_sems.at[1, k - 1, g],
            device_id={"dp": to}, device_id_type=MESH,
        )

    def cols_copy(k, g):
        to = lax.rem(c + k, n_cols)
        at = pl.ds(g * part, part)
        return pltpu.make_async_remote_copy(
            src_ref=low_cols.at[to, at], dst_ref=got_cols.at[k - 1, at],
            send_sem=cols_sems.at[0, k - 1, g], recv_sem=cols_sems.at[1, k - 1, g],
            device_id={"cols": to}, device_id_type=MESH,
        )

    def rows_copy(to):
        return pltpu.make_async_remote_copy(
            src_ref=low_rows.at[to], dst_ref=got_rows.at[r],
            send_sem=rows_sems.at[0, to], recv_sem=rows_sems.at[1, r],
            device_id={"rows": to}, device_id_type=MESH,
        )

    def rows_arrival(source):
        return pltpu.make_async_remote_copy(
            src_ref=low_rows.at[source], dst_ref=got_rows.at[source],
            send_sem=rows_sems.at[0, source], recv_sem=rows_sems.at[1, source],
            device_id={"rows": source}, device_id_type=MESH,
        )

    def product(g):
        at = slice(g * part, (g + 1) * part)
        left = att_t[at]
        for j in range(n_cols):
            for e in range(n_dp):
                first = (j * n_dp + e) * block_c
                term = mm(left, og[:, first : first + block_c], 1, 0)
                slab[e, j, at] = term
                slab_low[e, j, at] = term.astype(BF16)
        for k in range(1, n_dp):
            dp_copy(k, g).start()

    def sum_dp(g):
        at = slice(g * part, (g + 1) * part)
        for k in range(1, n_dp):
            dp_copy(k, g).wait()
        for j in range(n_cols):
            total = slab[d, j, at]
            for k in range(1, n_dp):
                total = total + got_dp[k - 1, j, at].astype(F32)
            slab[d, j, at] = total
            low_cols[j, at] = total.astype(BF16)
        for k in range(1, n_cols):
            cols_copy(k, g).start()

    def sum_cols(g):
        at = slice(g * part, (g + 1) * part)
        for k in range(1, n_cols):
            cols_copy(k, g).wait()
        total = slab[d, c, at]
        for k in range(1, n_cols):
            total = total + got_cols[k - 1, at].astype(F32)
        slab[d, c, at] = total
        for i in range(part // rows_c):
            to = g * part // rows_c + i
            low_rows[to] = total[i * rows_c : (i + 1) * rows_c].astype(BF16)
            pl.when(r != to)(lambda to=to: rows_copy(to).start())

    def send_rims(g):
        at = slice(g * part, (g + 1) * part)
        for k in range(2):
            rim_out[0, k, :, at] = acc[k, :edge, at].astype(BF16)
            rim_out[1, k, :, at] = acc[k, edge + tokens :, at].astype(BF16)
            for s in range(sides):
                srim_out[s, k, :, at] = sacc[s, k, :, at].astype(BF16)
        start_all(rim_copy, g, rim_send, rim_recv)

    scatters = [scatter(s) for s in range(sides)]

    def add_rims(g):
        at = slice(g * part, (g + 1) * part)
        wait_all(rim_copy, g, rim_send, rim_recv)
        for k in range(2):
            own = acc[k, edge : edge + tokens, at]
            for s in range(sides):
                own = own + mm(scatters[s], srim_in[s, k, :, at], 1, 0)
            acc[k, edge : edge + tokens, at] = own
            acc[k, edge : 2 * edge, at] += rim_in[0, k, :, at].astype(F32)
            acc[k, tokens : edge + tokens, at] += rim_in[1, k, :, at].astype(F32)
            kvg_ref[k, :, at] = acc[k, edge : edge + tokens, at].astype(BF16)

    for g in range(chunks):
        wait_all(halo_copy, g, halo_send, halo_recv)
        lax.fori_loop(g * CHUNK, (g + 1) * CHUNK, attend, 0)
        send_rims(g)
        product(g)
        if g >= 1:
            sum_dp(g - 1)
        if g >= 2:
            sum_cols(g - 2)
    out_ref[...] = mm(att_t[...], w_ref[...], 0, 0).astype(BF16)
    sum_dp(chunks - 1)
    if chunks >= 2:
        sum_cols(chunks - 2)
    for g in range(chunks - 1):
        add_rims(g)
    sum_cols(chunks - 1)
    add_rims(chunks - 1)

    for source in range(n_rows):
        def finish(source=source):
            rows_arrival(source).wait_recv()
            rows_copy(source).wait_send()
        pl.when(r != source)(finish)
    total = slab[d, c, pl.ds(pl.multiple_of(r * rows_c, rows_c), rows_c)]
    for source in range(n_rows):
        total = total + got_rows[source].astype(F32)
    wg_ref[...] = total * (1.0 / math.sqrt(image_h * image_w * n_dp))


def local(n_rows, n_cols, n_dp, queries, keys_values, out_weight, out_grad):
    tile_h, tile_w, width = queries.shape[1:]
    tokens = tile_h * tile_w
    sides = 1 if n_cols == 2 else 2
    blocks = tile_h // QB
    pairs = width // PAIR
    edge = RAD * tile_w
    grown = tokens + 2 * edge
    sgrown = GROUP * (blocks + 2)
    seen = (QB + 2 * RAD) * tile_w + sides * 3 * GROUP
    step = QB * tile_w
    block_c = width // (n_cols * n_dp)
    rows_c = width // n_rows
    links = 2 + 3 * sides
    chunks = pairs // CHUNK
    vmem = pl.BlockSpec(memory_space=pltpu.VMEM)
    dma = pltpu.SemaphoreType.DMA
    out, dq, kvg, wg = pl.pallas_call(
        functools.partial(kernel, tile_h, tile_w, n_rows, n_cols, n_dp),
        out_shape=(
            jax.ShapeDtypeStruct((tokens, width), BF16),
            jax.ShapeDtypeStruct((tokens, width), BF16),
            jax.ShapeDtypeStruct((2, tokens, width), BF16),
            jax.ShapeDtypeStruct((rows_c, block_c), F32),
        ),
        in_specs=[vmem] * 4,
        out_specs=(vmem,) * 4,
        scratch_shapes=[
            pltpu.VMEM((2, grown, width), BF16),
            pltpu.VMEM((sides, 2, sgrown, width), BF16),
            pltpu.VMEM((sides, 2, tile_h * RAD, width), BF16),
            pltpu.VMEM((2, grown, width), F32),
            pltpu.VMEM((sides, 2, sgrown, width), F32),
            pltpu.VMEM((blocks, seen, step), F32),
            pltpu.VMEM((width, tokens), BF16),
            pltpu.VMEM((tokens, width), BF16),
            pltpu.VMEM((2, 2, edge, width), BF16),
            pltpu.VMEM((2, 2, edge, width), BF16),
            pltpu.VMEM((sides, 2, sgrown, width), BF16),
            pltpu.VMEM((sides, 2, sgrown, width), BF16),
            pltpu.VMEM((n_dp, n_cols, width, block_c), F32),
            pltpu.VMEM((n_dp, n_cols, width, block_c), BF16),
            pltpu.VMEM((n_dp - 1, n_cols, width, block_c), BF16),
            pltpu.VMEM((n_cols, width, block_c), BF16),
            pltpu.VMEM((n_cols - 1, width, block_c), BF16),
            pltpu.VMEM((n_rows, rows_c, block_c), BF16),
            pltpu.VMEM((n_rows, rows_c, block_c), BF16),
            dma((links, chunks)), dma((links, chunks)), dma((links, chunks)), dma((links, chunks)),
            dma((2, n_dp - 1, chunks)), dma((2, n_cols - 1, chunks)), dma((2, n_rows)),
        ],
        compiler_params=pltpu.CompilerParams(
            collective_id=0, has_side_effects=True, vmem_limit_bytes=60 * 2**20
        ),
    )(
        queries.reshape(tokens, width),
        keys_values.reshape(2, tokens, width),
        out_weight,
        out_grad.reshape(tokens, width),
    )
    return (
        out.reshape(queries.shape),
        dq.reshape(queries.shape),
        kvg.reshape(keys_values.shape),
        wg,
    )


def solution(mesh):
    in_specs = (
        P("dp", "rows", "cols", None),
        P(None, "dp", "rows", "cols", None),
        P(),
        P("dp", "rows", "cols", None),
    )
    out_specs = (
        P("dp", "rows", "cols", None),
        P("dp", "rows", "cols", None),
        P(None, "dp", "rows", "cols", None),
        P("rows", ("cols", "dp")),
    )
    sizes = (mesh.shape["rows"], mesh.shape["cols"], mesh.shape["dp"])
    return jax.shard_map(
        functools.partial(local, *sizes),
        mesh=mesh, in_specs=in_specs, out_specs=out_specs, check_vma=False,
    )
```

```python
import functools
import math

import jax
import jax.numpy as jnp
from jax import lax
from jax.experimental import pallas as pl
from jax.experimental.pallas import tpu as pltpu
from jax.sharding import PartitionSpec as P

NH = 16
HD = 64
RAD = 6
WIN = 13
QB = 8
PAIR = 2 * HD
CHUNK = 1
GROUP = QB * RAD
MESH = pl.DeviceIdType.MESH
F32 = jnp.float32
BF16 = jnp.bfloat16


def mm(a, b, ca, cb):
    return lax.dot_general(a, b, (((ca,), (cb,)), ((), ())), preferred_element_type=F32)


def kernel(
    tile_h, tile_w, n_rows, n_cols, n_dp,
    q_ref, kv_ref, w_ref, og_ref,
    out_ref, dq_ref, kvg_ref, wg_ref,
    main, strip, sstrip, acc, sacc, bias, att_t, d_att,
    rim_out, rim_in, srim_out, srim_in,
    slab, slab_low, got_dp, low_cols, got_cols, low_rows, got_rows,
    halo_send, halo_recv, rim_send, rim_recv, dp_sems, cols_sems, rows_sems,
):
    sides = strip.shape[0]
    blocks = tile_h // QB
    tokens = tile_h * tile_w
    width = q_ref.shape[1]
    pairs = width // PAIR
    edge = RAD * tile_w
    span = (QB + 2 * RAD) * tile_w
    sspan = 3 * GROUP
    step = QB * tile_w
    image_h, image_w = tile_h * n_rows, tile_w * n_cols
    scale = 1.0 / math.sqrt(HD)
    r, c, d = lax.axis_index("rows"), lax.axis_index("cols"), lax.axis_index("dp")

    links = [(-1, None), (1, None)] + [(dr, s) for s in range(sides) for dr in (0, -1, 1)]

    def partner(dr, s):
        if s is None:
            col = c
        elif sides == 1:
            col = 1 - c
        else:
            col = c + (2 * s - 1)
        return {"rows": r + dr, "cols": col}

    def there(dr, s):
        ok = None
        if dr:
            ok = r > 0 if dr < 0 else r < n_rows - 1
        if s is not None and sides == 2:
            side_ok = c > 0 if s == 0 else c < n_cols - 1
            ok = side_ok if ok is None else ok & side_ok
        return ok

    def guarded(dr, s, action):
        ok = there(dr, s)
        if ok is None:
            action()
        else:
            pl.when(ok)(action)

    def slot(s):
        return 0 if sides == 1 else 1 - s

    def starts_at(s):
        if sides == 1:
            return (1 - c) * (tile_w - RAD)
        return 0 if s == 0 else tile_w - RAD

    barrier = pltpu.get_barrier_semaphore()
    for k in range(1, n_rows):
        pl.semaphore_signal(barrier, 1, device_id={"rows": lax.rem(r + k, n_rows)}, device_id_type=MESH)
    for k in range(1, n_cols):
        pl.semaphore_signal(barrier, 1, device_id={"cols": lax.rem(c + k, n_cols)}, device_id_type=MESH)
    for k in range(1, n_dp):
        pl.semaphore_signal(barrier, 1, device_id={"dp": lax.rem(d + k, n_dp)}, device_id_type=MESH)
    greeted = n_rows + n_cols + n_dp - 3
    for dr, s in links:
        if dr and s is not None:
            def greet(dr=dr, s=s):
                pl.semaphore_signal(barrier, 1, device_id=partner(dr, s), device_id_type=MESH)
            guarded(dr, s, greet)
            greeted = greeted + there(dr, s).astype(jnp.int32)

    strip_tokens = tile_h * RAD

    def pick(n, s):
        token = lax.broadcasted_iota(jnp.int32, (n, tokens), 0)
        row = (token * 10923) >> 16
        col = token - row * RAD
        place = row * tile_w + col + starts_at(s)
        return (place == lax.broadcasted_iota(jnp.int32, (n, tokens), 1)).astype(F32).astype(BF16)

    def scatter(s):
        shape = (tokens, GROUP * (blocks + 2))
        token = lax.broadcasted_iota(jnp.int32, shape, 1)
        row = (token * 10923) >> 16
        col = token - row * RAD
        row = row - jnp.where(row < QB, 0, jnp.where(row < QB + tile_h, QB, 2 * QB))
        place = row * tile_w + col + starts_at(s)
        return (place == lax.broadcasted_iota(jnp.int32, shape, 0)).astype(F32).astype(BF16)

    for s in range(sides):
        chosen = pick(strip_tokens, s)
        for k in range(2):
            sstrip[s, k] = mm(chosen, kv_ref[k], 1, 0).astype(BF16)

    pl.semaphore_wait(barrier, greeted)

    chunks = pairs // CHUNK
    part = CHUNK * PAIR

    def halo_copy(index, at):
        dr, s = links[index]
        if s is None:
            if dr < 0:
                return kv_ref.at[:, pl.ds(0, edge), at], main.at[:, pl.ds(edge + tokens, edge), at]
            return kv_ref.at[:, pl.ds(tokens - edge, edge), at], main.at[:, pl.ds(0, edge), at]
        own, far = sstrip.at[s], strip.at[slot(s)]
        if dr == 0:
            return own.at[:, :, at], far.at[:, pl.ds(GROUP, strip_tokens), at]
        if dr < 0:
            return own.at[:, pl.ds(0, GROUP), at], far.at[:, pl.ds(GROUP + strip_tokens, GROUP), at]
        return own.at[:, pl.ds(strip_tokens - GROUP, GROUP), at], far.at[:, pl.ds(0, GROUP), at]

    def rim_copy(index, at):
        dr, s = links[index]
        if s is None:
            way = 0 if dr < 0 else 1
            return rim_out.at[way, :, :, at], rim_in.at[1 - way, :, :, at]
        own, far = srim_out.at[s], srim_in.at[slot(s)]
        if dr == 0:
            which = pl.ds(GROUP, strip_tokens)
            return own.at[:, which, at], far.at[:, which, at]
        first, last = pl.ds(0, GROUP), pl.ds(GROUP + strip_tokens, GROUP)
        if dr < 0:
            return own.at[:, first, at], far.at[:, last, at]
        return own.at[:, last, at], far.at[:, first, at]

    def mirror(index):
        dr, s = links[index]
        return links.index((-dr, None if s is None else (s if sides == 1 else 1 - s)))

    def remote(copy, index, g, send, recv):
        src, dst = copy(index, pl.ds(g * part, part))
        return pltpu.make_async_remote_copy(
            src_ref=src, dst_ref=dst, send_sem=send.at[index, g], recv_sem=recv.at[mirror(index), g],
            device_id=partner(*links[index]), device_id_type=MESH,
        )

    def start_all(copy, g, send, recv):
        for index in range(len(links)):
            guarded(*links[index], lambda index=index: remote(copy, index, g, send, recv).start())

    def wait_all(copy, g, send, recv):
        for index in range(len(links)):
            def action(index=index):
                src, dst = copy(mirror(index), pl.ds(g * part, part))
                pltpu.make_async_remote_copy(
                    src_ref=src, dst_ref=dst, send_sem=send.at[index, g], recv_sem=recv.at[index, g],
                    device_id=partner(*links[index]), device_id_type=MESH,
                ).wait_recv()
                remote(copy, index, g, send, recv).wait_send()
            guarded(*links[index], action)

    for g in range(chunks):
        start_all(halo_copy, g, halo_send, halo_recv)

    for index in range(len(links)):
        ok = there(*links[index])
        if ok is not None:
            def clear(index=index):
                dst = halo_copy(mirror(index), pl.ds(0, width))[1]
                dst[...] = jnp.zeros(dst.shape, BF16)
                dst = rim_copy(mirror(index), pl.ds(0, width))[1]
                dst[...] = jnp.zeros(dst.shape, BF16)
            pl.when(jnp.logical_not(ok))(clear)

    for k in range(2):
        main[k, edge : edge + tokens] = kv_ref[k]
    got_rows[r] = jnp.zeros(got_rows.shape[1:], BF16)

    d_att[...] = mm(og_ref[...], w_ref[...], 1, 1).astype(BF16)
    acc[...] = jnp.zeros(acc.shape, F32)
    sacc[...] = jnp.zeros(sacc.shape, F32)

    def put_bias(b, at, rows, cols, n):
        lane = lax.broadcasted_iota(jnp.int32, (n, step), 1)
        q_row = r * tile_h + b * QB + lane // tile_w
        q_col = c * tile_w + lane % tile_w
        first_r = jnp.clip(q_row - RAD, 0, image_h - WIN)
        first_c = jnp.clip(q_col - RAD, 0, image_w - WIN)
        ok = (rows >= first_r) & (rows < first_r + WIN) & (cols >= first_c) & (cols < first_c + WIN)
        bias[b, at : at + n] = jnp.where(ok, 0.0, -1e30)

    for b in range(blocks):
        token = lax.broadcasted_iota(jnp.int32, (span, step), 0)
        put_bias(b, 0, r * tile_h + b * QB - RAD + token // tile_w, c * tile_w + token % tile_w, span)
        token = lax.broadcasted_iota(jnp.int32, (sspan, step), 0)
        row = (token * 10923) >> 16
        for s in range(sides):
            if sides == 1:
                first = c * tile_w + jnp.where(c == 0, tile_w, -RAD)
            else:
                first = c * tile_w + (tile_w if s else -RAD)
            put_bias(
                b, span + s * sspan, r * tile_h + (b - 1) * QB + row, first + token - row * RAD, sspan
            )

    def lanes(p):
        return pl.ds(pl.multiple_of(p * PAIR, PAIR), PAIR)

    def keys_of(k, b, p):
        parts = [main[k, step * b : step * b + span, lanes(p)]]
        for s in range(sides):
            parts.append(strip[s, k, GROUP * b : GROUP * b + sspan, lanes(p)])
        return jnp.concatenate(parts, axis=0)

    def split_heads(x):
        low_head = lax.broadcasted_iota(jnp.int32, x.shape, 1) < HD
        wide = x.astype(F32)
        return jnp.concatenate(
            [jnp.where(low_head, wide, 0.0), jnp.where(low_head, 0.0, wide)], axis=0
        ).astype(BF16)

    def queries_of(b, p):
        return split_heads(q_ref[step * b : step * (b + 1), lanes(p)].astype(F32) * scale)

    def own_heads(x):
        return jnp.concatenate([x[:HD, :step], x[HD:, step:]], axis=0)

    def attend(p, carry):
        for b in range(blocks):
            here = slice(step * b, step * (b + 1))
            keys, values = keys_of(0, b, p), keys_of(1, b, p)
            q_two = queries_of(b, p)
            d_blk = d_att[here, lanes(p)]
            d_two = split_heads(d_blk)
            hidden = bias[b]
            scores = mm(keys, q_two, 1, 1) + jnp.concatenate([hidden, hidden], axis=1)
            expd = jnp.exp(scores - jnp.max(scores, axis=0, keepdims=True))
            full = expd * (1.0 / jnp.sum(expd, axis=0, keepdims=True))
            low = full.astype(BF16)
            att = own_heads(mm(values, low, 0, 0)).astype(BF16)
            att_t[lanes(p), here] = att
            both = d_blk.astype(F32).T * att.astype(F32)
            delta = jnp.concatenate(
                [
                    jnp.sum(both[:HD], axis=0, keepdims=True),
                    jnp.sum(both[HD:], axis=0, keepdims=True),
                ],
                axis=1,
            )
            dscores = (full * (mm(values, d_two, 1, 1) - delta)).astype(BF16)
            dq = own_heads(mm(keys, dscores, 0, 0)) * scale
            dq_ref[here, lanes(p)] = dq.T.astype(BF16)
            for k, grad in ((0, mm(dscores, q_two, 1, 0)), (1, mm(low, d_two, 1, 0))):
                acc[k, step * b : step * b + span, lanes(p)] += grad[:span]
                for s in range(sides):
                    at = span + s * sspan
                    sacc[s, k, GROUP * b : GROUP * b + sspan, lanes(p)] += grad[at : at + sspan]
        return carry

    block_c = slab.shape[3]
    rows_c = width // n_rows
    og = og_ref[...]

    def dp_copy(k, g):
        to = lax.rem(d + k, n_dp)
        at = pl.ds(g * part, part)
        return pltpu.make_async_remote_copy(
            src_ref=slab_low.at[to, :, at], dst_ref=got_dp.at[k - 1, :, at],
            send_sem=dp_sems.at[0, k - 1, g], recv_sem=dp_sems.at[1, k - 1, g],
            device_id={"dp": to}, device_id_type=MESH,
        )

    def cols_copy(k, g):
        to = lax.rem(c + k, n_cols)
        at = pl.ds(g * part, part)
        return pltpu.make_async_remote_copy(
            src_ref=low_cols.at[to, at], dst_ref=got_cols.at[k - 1, at],
            send_sem=cols_sems.at[0, k - 1, g], recv_sem=cols_sems.at[1, k - 1, g],
            device_id={"cols": to}, device_id_type=MESH,
        )

    def rows_copy(to):
        return pltpu.make_async_remote_copy(
            src_ref=low_rows.at[to], dst_ref=got_rows.at[r],
            send_sem=rows_sems.at[0, to], recv_sem=rows_sems.at[1, r],
            device_id={"rows": to}, device_id_type=MESH,
        )

    def rows_arrival(source):
        return pltpu.make_async_remote_copy(
            src_ref=low_rows.at[source], dst_ref=got_rows.at[source],
            send_sem=rows_sems.at[0, source], recv_sem=rows_sems.at[1, source],
            device_id={"rows": source}, device_id_type=MESH,
        )

    def product(g):
        at = slice(g * part, (g + 1) * part)
        left = att_t[at]
        for j in range(n_cols):
            for e in range(n_dp):
                first = (j * n_dp + e) * block_c
                term = mm(left, og[:, first : first + block_c], 1, 0)
                slab[e, j, at] = term
                slab_low[e, j, at] = term.astype(BF16)
        for k in range(1, n_dp):
            dp_copy(k, g).start()

    def sum_dp(g):
        at = slice(g * part, (g + 1) * part)
        for k in range(1, n_dp):
            dp_copy(k, g).wait()
        for j in range(n_cols):
            total = slab[d, j, at]
            for k in range(1, n_dp):
                total = total + got_dp[k - 1, j, at].astype(F32)
            slab[d, j, at] = total
            low_cols[j, at] = total.astype(BF16)
        for k in range(1, n_cols):
            cols_copy(k, g).start()

    def sum_cols(g):
        at = slice(g * part, (g + 1) * part)
        for k in range(1, n_cols):
            cols_copy(k, g).wait()
        total = slab[d, c, at]
        for k in range(1, n_cols):
            total = total + got_cols[k - 1, at].astype(F32)
        slab[d, c, at] = total
        for i in range(part // rows_c):
            to = g * part // rows_c + i
            low_rows[to] = total[i * rows_c : (i + 1) * rows_c].astype(BF16)
            pl.when(r != to)(lambda to=to: rows_copy(to).start())

    def send_rims(g):
        at = slice(g * part, (g + 1) * part)
        for k in range(2):
            rim_out[0, k, :, at] = acc[k, :edge, at].astype(BF16)
            rim_out[1, k, :, at] = acc[k, edge + tokens :, at].astype(BF16)
            for s in range(sides):
                srim_out[s, k, :, at] = sacc[s, k, :, at].astype(BF16)
        start_all(rim_copy, g, rim_send, rim_recv)

    scatters = [scatter(s) for s in range(sides)]

    def add_rims(g):
        at = slice(g * part, (g + 1) * part)
        wait_all(rim_copy, g, rim_send, rim_recv)
        for k in range(2):
            own = acc[k, edge : edge + tokens, at]
            for s in range(sides):
                own = own + mm(scatters[s], srim_in[s, k, :, at], 1, 0)
            acc[k, edge : edge + tokens, at] = own
            acc[k, edge : 2 * edge, at] += rim_in[0, k, :, at].astype(F32)
            acc[k, tokens : edge + tokens, at] += rim_in[1, k, :, at].astype(F32)
            kvg_ref[k, :, at] = acc[k, edge : edge + tokens, at].astype(BF16)

    for g in range(chunks):
        wait_all(halo_copy, g, halo_send, halo_recv)
        lax.fori_loop(g * CHUNK, (g + 1) * CHUNK, attend, 0)
        send_rims(g)
        product(g)
        if g >= 1:
            sum_dp(g - 1)
        if g >= 2:
            sum_cols(g - 2)
    out_ref[...] = mm(att_t[...], w_ref[...], 0, 0).astype(BF16)
    sum_dp(chunks - 1)
    if chunks >= 2:
        sum_cols(chunks - 2)
    for g in range(chunks - 1):
        add_rims(g)
    sum_cols(chunks - 1)
    add_rims(chunks - 1)

    for source in range(n_rows):
        def finish(source=source):
            rows_arrival(source).wait_recv()
            rows_copy(source).wait_send()
        pl.when(r != source)(finish)
    total = slab[d, c, pl.ds(pl.multiple_of(r * rows_c, rows_c), rows_c)]
    for source in range(n_rows):
        total = total + got_rows[source].astype(F32)
    wg_ref[...] = total * (1.0 / math.sqrt(image_h * image_w * n_dp))


def local(n_rows, n_cols, n_dp, queries, keys_values, out_weight, out_grad):
    tile_h, tile_w, width = queries.shape[1:]
    tokens = tile_h * tile_w
    sides = 1 if n_cols == 2 else 2
    blocks = tile_h // QB
    pairs = width // PAIR
    edge = RAD * tile_w
    grown = tokens + 2 * edge
    sgrown = GROUP * (blocks + 2)
    seen = (QB + 2 * RAD) * tile_w + sides * 3 * GROUP
    step = QB * tile_w
    block_c = width // (n_cols * n_dp)
    rows_c = width // n_rows
    links = 2 + 3 * sides
    chunks = pairs // CHUNK
    vmem = pl.BlockSpec(memory_space=pltpu.VMEM)
    dma = pltpu.SemaphoreType.DMA
    out, dq, kvg, wg = pl.pallas_call(
        functools.partial(kernel, tile_h, tile_w, n_rows, n_cols, n_dp),
        out_shape=(
            jax.ShapeDtypeStruct((tokens, width), BF16),
            jax.ShapeDtypeStruct((tokens, width), BF16),
            jax.ShapeDtypeStruct((2, tokens, width), BF16),
            jax.ShapeDtypeStruct((rows_c, block_c), F32),
        ),
        in_specs=[vmem] * 4,
        out_specs=(vmem,) * 4,
        scratch_shapes=[
            pltpu.VMEM((2, grown, width), BF16),
            pltpu.VMEM((sides, 2, sgrown, width), BF16),
            pltpu.VMEM((sides, 2, tile_h * RAD, width), BF16),
            pltpu.VMEM((2, grown, width), F32),
            pltpu.VMEM((sides, 2, sgrown, width), F32),
            pltpu.VMEM((blocks, seen, step), F32),
            pltpu.VMEM((width, tokens), BF16),
            pltpu.VMEM((tokens, width), BF16),
            pltpu.VMEM((2, 2, edge, width), BF16),
            pltpu.VMEM((2, 2, edge, width), BF16),
            pltpu.VMEM((sides, 2, sgrown, width), BF16),
            pltpu.VMEM((sides, 2, sgrown, width), BF16),
            pltpu.VMEM((n_dp, n_cols, width, block_c), F32),
            pltpu.VMEM((n_dp, n_cols, width, block_c), BF16),
            pltpu.VMEM((n_dp - 1, n_cols, width, block_c), BF16),
            pltpu.VMEM((n_cols, width, block_c), BF16),
            pltpu.VMEM((n_cols - 1, width, block_c), BF16),
            pltpu.VMEM((n_rows, rows_c, block_c), BF16),
            pltpu.VMEM((n_rows, rows_c, block_c), BF16),
            dma((links, chunks)), dma((links, chunks)), dma((links, chunks)), dma((links, chunks)),
            dma((2, n_dp - 1, chunks)), dma((2, n_cols - 1, chunks)), dma((2, n_rows)),
        ],
        compiler_params=pltpu.CompilerParams(
            collective_id=0, has_side_effects=True, vmem_limit_bytes=60 * 2**20
        ),
    )(
        queries.reshape(tokens, width),
        keys_values.reshape(2, tokens, width),
        out_weight,
        out_grad.reshape(tokens, width),
    )
    return (
        out.reshape(queries.shape),
        dq.reshape(queries.shape),
        kvg.reshape(keys_values.shape),
        wg,
    )


def solution(mesh):
    in_specs = (
        P("dp", "rows", "cols", None),
        P(None, "dp", "rows", "cols", None),
        P(),
        P("dp", "rows", "cols", None),
    )
    out_specs = (
        P("dp", "rows", "cols", None),
        P("dp", "rows", "cols", None),
        P(None, "dp", "rows", "cols", None),
        P("rows", ("cols", "dp")),
    )
    sizes = (mesh.shape["rows"], mesh.shape["cols"], mesh.shape["dp"])
    return jax.shard_map(
        functools.partial(local, *sizes),
        mesh=mesh, in_specs=in_specs, out_specs=out_specs, check_vma=False,
    )
```
